32 devices in a mesh: seq: 16 (over z, y, x), tp: 2 (over core).
Axes of the slice: x: 2, y: 2, z: 4, core: 2. Of those that a mesh axis runs over, the one named last changes fastest.
Arguments:
- queries: bfloat16 [8192, 4096], P('seq', 'tp'), may hold values from -6 to 6
- keys: bfloat16 [8192, 4096], P('seq', 'tp'), may hold values from -6 to 6
- values: bfloat16 [8192, 4096], P('seq', 'tp'), may hold values from -60 to 60
- block_mask: int32 [32, 2], P('seq'), may hold values 0 or 1
- gain: float32 [4096], P('tp'), may hold values from 0.5 to 1.5
Outputs:
- attended: bfloat16 [8192, 4096], P('seq', 'tp')
The draws below stay inside these ranges and needn't reach their ends.
All inputs are finite; a program needn't handle non-finite values. No bound on the sum of `block_mask` on one device may be relied on, other than what follows from the above.
Results may differ from the reference program's by a relative error of at most 0.005.
Values sent between devices are 32-bit elements; how exact they have to be, the bound alone decides.
A program may use at most 320 MiB of HBM per device.

```python
import jax
import jax.numpy as jnp
from jax import lax

HEADS = 32
HD = 128
BLOCK = 256
TOK_DEV = 512
WIDTH = 4096
TOKENS = 8192
NB = 2
SEQ_BLOCKS = 32
N_SEQ = 16


def draw_values(key, part):
    head_index = jnp.arange(HEADS * HD) // HD
    fraction = head_index.astype(jnp.float32) / max(HEADS - 1, 1)
    base = jnp.clip(jax.random.normal(key, (TOKENS, HEADS * HD), jnp.float32), -6.0, 6.0)
    scale = 10.0 ** fraction
    return (base * scale[None, :]).astype(jnp.bfloat16)


def with_ends(result, key, smallest, top_value):
    index_at = [jax.random.randint(jax.random.fold_in(key, axis), (), 0, length) for axis, length in enumerate(result.shape)]
    main_axis = result.shape.index(max(result.shape))
    beside = index_at[:main_axis] + [(index_at[main_axis] + 1) % result.shape[main_axis]] + index_at[main_axis + 1:]
    return result.at[tuple(index_at)].set(smallest).at[tuple(beside)].set(top_value)


def block_scale(stream_key, shape, pieces, low, top_value):
    level, own = 1.0, jax.random.fold_in(stream_key, 6)
    for position, shards_of in pieces:
        heights = jnp.exp(jax.random.uniform(jax.random.fold_in(own, position), (shards_of,), jnp.float32, low / len(pieces), top_value / len(pieces)))
        level = level * jnp.repeat(heights, shape[position] // shards_of).reshape([-1 if axis == position else 1 for axis in range(len(shape))])
    return level


def gaussian(key, extent, deviation, reach, cuts=(), kind=jnp.bfloat16):
    result = jax.random.normal(key, extent, jnp.float32) * deviation
    if len(cuts) > 0:
        result = block_scale(key, extent, cuts, -0.22, 0.18) * result
    return jnp.clip(result, min=-reach, max=reach).astype(kind)


def setup_inputs(seed: int = 0) -> dict:
    key_list = jax.random.split(jax.random.key(seed), 6)
    queries = gaussian(key_list[0], (TOKENS, WIDTH), 1.0, 6.0, ((0, 16), (1, 2)))
    keys = gaussian(key_list[1], (TOKENS, WIDTH), 1.0, 6.0, ((0, 16), (1, 2)))
    values = draw_values(jax.random.fold_in(key_list[5], 71), 0)
    block_mask = with_ends((jax.random.randint(key_list[3], (SEQ_BLOCKS, NB), 0, 2) < 1).astype(jnp.int32), jax.random.fold_in(key_list[3], 1), 0, 1)
    gain = jnp.clip(1.0 + 0.1 * jax.random.normal(key_list[4], (WIDTH,), jnp.float32), 0.5, 1.5)
    return dict(queries=queries, keys=keys, values=values, block_mask=block_mask, gain=gain)


def allowed_table(table):
    count = table.shape[0]
    block_of = jnp.arange(TOK_DEV) // BLOCK
    expanded = jnp.broadcast_to(table[:, None, :, None], (count, BLOCK, count, BLOCK)).reshape(TOK_DEV, TOK_DEV)
    same = block_of[:, None] == block_of[None, :]
    lower = block_of[:, None] > block_of[None, :]
    return same | lower & (expanded == 1)

def reference(queries, keys, values, block_mask, gain):
    qs = queries.reshape(N_SEQ, TOK_DEV, HEADS, HD)
    ks = keys.reshape(N_SEQ, TOK_DEV, HEADS, HD)
    vs = values.reshape(N_SEQ, TOK_DEV, HEADS, HD)
    tables = block_mask.reshape(N_SEQ, NB, NB)
    gains = gain.astype(jnp.float32)

    def shard_step(prefix, item):
        qpart, kpart, vpart, table = item
        qf = qpart.astype(jnp.float32)
        kf = kpart.astype(jnp.float32)
        vf = vpart.astype(jnp.float32)
        local_state = jnp.einsum('thd,the->hde', kf, vf)
        scores = jnp.einsum('thd,uhd->htu', qf, kf)
        allowed = allowed_table(table)
        weights = lax.optimization_barrier(jnp.where(allowed[None], scores, 0.0).astype(jnp.bfloat16))
        local = jnp.einsum('htu,uhe->the', weights.astype(jnp.float32), vf)
        carried = lax.optimization_barrier(prefix.astype(jnp.bfloat16))
        cross = jnp.einsum('thd,hde->the', qf, carried.astype(jnp.float32))
        mixed = (local + cross).reshape(TOK_DEV, HEADS * HD)
        mean_square = lax.optimization_barrier(jnp.mean(mixed * mixed, axis=1, keepdims=True))
        attended = (mixed * lax.rsqrt(mean_square + 1e-06) * gains[None, :]).astype(jnp.bfloat16)
        return (prefix + local_state, attended)
    start = jnp.zeros((HEADS, HD, HD), jnp.float32)
    _, outputs = lax.scan(shard_step, start, (qs, ks, vs, tables))
    return outputs.reshape(TOKENS, HEADS * HD)
```

```python
import functools

import jax
import jax.numpy as jnp
from jax import lax
from jax.experimental import pallas as pl
from jax.experimental.pallas import tpu as pltpu
from jax.sharding import PartitionSpec as P

HD = 128
BLOCK = 256
HC = 2
MESH = pl.DeviceIdType.MESH
F32 = jnp.float32


def kernel(
    n_seq, n_tp,
    q_hbm, k_hbm, v_hbm, mask_ref, gain_ref, out_hbm,
    q, k, v, mixed, outv,
    own, from_x, row, from_y, from_z, to_z, squares, other_squares,
    load_sem, x_send, x_recv, y_send, y_recv, z_send, z_recv, t_send, t_recv, out_sem,
):
    tokens, width = q.shape
    heads = width // HD
    chunks = heads // HC
    cw = HC * HD
    nb = tokens // BLOCK
    planes = n_seq // 4
    me = lax.axis_index("seq")
    core = lax.axis_index("tp")
    xi = lax.rem(me, 2)
    yi = lax.rem(me // 2, 2)
    zi = me // 4
    x_peer = me + 1 - 2 * xi
    y_peer = me + 2 - 4 * yi

    def cols(c):
        return pl.ds(pl.multiple_of(c * cw, cw), cw)

    def load(which, hbm, vmem, c):
        return pltpu.make_async_copy(hbm.at[:, cols(c)], vmem.at[:, cols(c)], load_sem.at[which, c])

    @pl.loop(0, chunks)
    def _(c):
        load(0, k_hbm, k, c).start()
        load(1, v_hbm, v, c).start()

    @pl.loop(0, chunks)
    def _(c):
        load(2, q_hbm, q, c).start()

    barrier = pltpu.get_barrier_semaphore()
    pl.semaphore_signal(barrier, inc=1, device_id={"seq": x_peer}, device_id_type=MESH)
    pl.semaphore_signal(barrier, inc=1, device_id={"seq": y_peer}, device_id_type=MESH)
    pl.semaphore_signal(barrier, inc=1, device_id={"tp": 1 - core}, device_id_type=MESH)

    @pl.when(zi > 0)
    def _():
        pl.semaphore_signal(barrier, inc=1, device_id={"seq": me - 4}, device_id_type=MESH)

    @pl.when(zi < planes - 1)
    def _():
        pl.semaphore_signal(barrier, inc=1, device_id={"seq": me + 4}, device_id_type=MESH)

    def heads_of(c):
        return pl.ds(c * HC, HC)

    def remote(src, dst, send, recv, c, peer):
        return pltpu.make_async_remote_copy(
            src_ref=src.at[heads_of(c)], dst_ref=dst.at[heads_of(c)],
            send_sem=send.at[c], recv_sem=recv.at[c],
            device_id={"seq": peer}, device_id_type=MESH,
        )

    def x_copy(c):
        return remote(own, from_x, x_send, x_recv, c, x_peer)

    def y_copy(c):
        return remote(row, from_y, y_send, y_recv, c, y_peer)

    def z_copy(c):
        return remote(to_z, from_z, z_send, z_recv, c, me + 4)

    @pl.when(zi == 0)
    def _():
        from_z[...] = jnp.zeros_like(from_z)

    squares[...] = jnp.zeros_like(squares)

    below = (zi + planes - 1) // planes
    above = (2 * planes - 2 - zi) // planes
    pl.semaphore_wait(barrier, 3 + below + above)

    @pl.loop(0, chunks)
    def _(c):
        load(0, k_hbm, k, c).wait()
        load(1, v_hbm, v, c).wait()
        for j in range(HC):
            at = pl.ds(pl.multiple_of(c * cw + j * HD, HD), HD)
            own[c * HC + j] = lax.dot_general(
                k[:, at], v[:, at], (((0,), (0,)), ((), ())), preferred_element_type=F32
            )
        x_copy(c).start()

    def after_x(c):
        x_copy(c).wait_recv()
        at = heads_of(c)
        row[at] = own[at] + from_x[at]
        y_copy(c).start()

    def after_y(c):
        y_copy(c).wait_recv()

        @pl.when(zi > 0)
        def _():
            z_copy(c).wait_recv()

        @pl.when(zi < planes - 1)
        def _():
            at = heads_of(c)
            to_z[at] = row[at] + from_y[at] + from_z[at]
            z_copy(c).start()

    def local(c):
        load(2, q_hbm, q, c).wait()
        for j in range(HC):
            at = pl.ds(pl.multiple_of(c * cw + j * HD, HD), HD)
            for b in range(nb):
                rows = slice(b * BLOCK, (b + 1) * BLOCK)
                qb = q[rows, at]
                total = None
                for u in range(b + 1):
                    other = slice(u * BLOCK, (u + 1) * BLOCK)
                    scores = lax.dot_general(
                        qb, k[other, at], (((1,), (1,)), ((), ())), preferred_element_type=F32
                    )
                    if u < b:
                        scores = jnp.where(mask_ref[b, u] == 1, scores, 0.0)
                    part = jnp.dot(
                        scores.astype(jnp.bfloat16), v[other, at], preferred_element_type=F32
                    )
                    total = part if total is None else total + part
                mixed[rows, at] = total

    def cross(c):
        for j in range(HC):
            at = pl.ds(pl.multiple_of(c * cw + j * HD, HD), HD)
            h = c * HC + j
            zero = jnp.zeros((HD, HD), F32)
            prefix = (
                from_z[h]
                + jnp.where(yi == 1, from_y[h], zero)
                + jnp.where(xi == 1, from_x[h], zero)
            ).astype(jnp.bfloat16)
            whole = mixed[:, at] + jnp.dot(q[:, at], prefix, preferred_element_type=F32)
            mixed[:, at] = whole
            squares[...] += whole * whole

    @pl.loop(0, chunks + 2)
    def _(s):
        @pl.when(s < chunks)
        def _():
            after_x(s)

        @pl.when(jnp.logical_and(s >= 1, s < chunks + 1))
        def _():
            after_y(s - 1)

        @pl.when(s < chunks)
        def _():
            local(s)

        @pl.when(s >= 2)
        def _():
            cross(s - 2)

    tp_copy = pltpu.make_async_remote_copy(
        src_ref=squares, dst_ref=other_squares, send_sem=t_send, recv_sem=t_recv,
        device_id={"tp": 1 - core}, device_id_type=MESH,
    )
    tp_copy.start()

    @pl.loop(0, chunks)
    def _(c):
        x_copy(c).wait_send()
        y_copy(c).wait_send()

        @pl.when(zi < planes - 1)
        def _():
            z_copy(c).wait_send()

    tp_copy.wait()
    rows_out = 64

    def out_copy(r):
        at = pl.ds(pl.multiple_of(r * rows_out, rows_out), rows_out)
        return pltpu.make_async_copy(outv.at[at], out_hbm.at[at], out_sem.at[r])

    @pl.loop(0, tokens // rows_out)
    def _(r):
        at = pl.ds(pl.multiple_of(r * rows_out, rows_out), rows_out)
        total = jnp.sum(squares[at] + other_squares[at], axis=1, keepdims=True)
        scale = lax.rsqrt(total / (width * n_tp) + 1e-6)
        outv[at] = (mixed[at] * scale * gain_ref[...]).astype(jnp.bfloat16)
        out_copy(r).start()

    @pl.loop(0, tokens // rows_out)
    def _(r):
        out_copy(r).wait()


def body(n_seq, n_tp, queries, keys, values, block_mask, gain):
    tokens, width = queries.shape
    heads = width // HD
    chunks = heads // HC
    state = pltpu.VMEM((heads, HD, HD), F32)
    sems = pltpu.SemaphoreType.DMA
    return pl.pallas_call(
        functools.partial(kernel, n_seq, n_tp),
        out_shape=jax.ShapeDtypeStruct((tokens, width), jnp.bfloat16),
        in_specs=[pl.BlockSpec(memory_space=pl.ANY)] * 3
        + [pl.BlockSpec(memory_space=pltpu.SMEM), pl.BlockSpec(memory_space=pltpu.VMEM)],
        out_specs=pl.BlockSpec(memory_space=pl.ANY),
        scratch_shapes=[pltpu.VMEM((tokens, width), jnp.bfloat16)] * 3
        + [pltpu.VMEM((tokens, width), F32), pltpu.VMEM((tokens, width), jnp.bfloat16)]
        + [state] * 6
        + [pltpu.VMEM((tokens, HD), F32)] * 2
        + [sems((3, chunks))]
        + [sems((chunks,))] * 6
        + [sems, sems, sems((tokens // 64,))],
        compiler_params=pltpu.CompilerParams(
            collective_id=0, has_side_effects=True, vmem_limit_bytes=60 * 1024 * 1024
        ),
    )(queries, keys, values, block_mask, gain.reshape(1, width))


def solution(mesh):
    placed = (P("seq", "tp"), P("seq", "tp"), P("seq", "tp"), P("seq", None), P("tp"))
    return jax.shard_map(
        functools.partial(body, mesh.shape["seq"], mesh.shape["tp"]),
        mesh=mesh, in_specs=placed, out_specs=P("seq", "tp"), check_vma=False,
    )
```

```python
import functools

import jax
import jax.numpy as jnp
from jax import lax
from jax.experimental import pallas as pl
from jax.experimental.pallas import tpu as pltpu
from jax.sharding import PartitionSpec as P

HD = 128
BLOCK = 256
PAIR = 2
RETURN_LAG = 2
MESH = pl.DeviceIdType.MESH
F32 = jnp.float32


def kernel(
    n_seq, n_tp,
    q_hbm, k_hbm, v_hbm, mask_ref, gain_ref, out,
    q, k, v, mixed,
    own, from_x, row, from_y, from_z, to_z, to_back, back, squares, other_squares,
    load_sem, x_send, x_recv, y_send, y_recv, z_send, z_recv, b_send, b_recv, t_send, t_recv,
):
    tokens, width = q.shape
    heads = width // HD
    half = heads // 2
    nb = tokens // BLOCK
    planes = n_seq // 4
    me = lax.axis_index("seq")
    core = lax.axis_index("tp")
    xi = lax.rem(me, 2)
    yi = lax.rem(me // 2, 2)
    zi = me // 4
    x_peer = me + 1 - 2 * xi
    y_peer = me + 2 - 4 * yi
    mine = half * xi
    theirs = half - mine

    def head_cols(h, count=1):
        return pl.ds(pl.multiple_of(h * HD, HD), count * HD)

    def load(which, hbm, vmem, first, j):
        at = head_cols(first + j * PAIR, PAIR)
        return pltpu.make_async_copy(
            hbm.at[:, at], vmem.at[:, at], load_sem.at[which, first // PAIR + j]
        )

    for first in (theirs, mine):
        @pl.loop(0, half // PAIR)
        def _(j):
            load(0, k_hbm, k, first, j).start()
            load(1, v_hbm, v, first, j).start()

    @pl.loop(0, half // PAIR)
    def _(j):
        load(2, q_hbm, q, mine, j).start()
        load(2, q_hbm, q, theirs, j).start()

    barrier = pltpu.get_barrier_semaphore()
    pl.semaphore_signal(barrier, inc=1, device_id={"seq": x_peer}, device_id_type=MESH)
    pl.semaphore_signal(barrier, inc=1, device_id={"seq": y_peer}, device_id_type=MESH)
    pl.semaphore_signal(barrier, inc=1, device_id={"tp": 1 - core}, device_id_type=MESH)

    @pl.when(zi > 0)
    def _():
        pl.semaphore_signal(barrier, inc=1, device_id={"seq": me - 4}, device_id_type=MESH)

    @pl.when(zi < planes - 1)
    def _():
        pl.semaphore_signal(barrier, inc=1, device_id={"seq": me + 4}, device_id_type=MESH)

    def remote(src, at, dst, c, send, recv, peer):
        return pltpu.make_async_remote_copy(
            src_ref=src.at[at], dst_ref=dst.at[c], send_sem=send.at[c], recv_sem=recv.at[c],
            device_id={"seq": peer}, device_id_type=MESH,
        )

    def x_copy(c):
        return remote(own, theirs + c, from_x, c, x_send, x_recv, x_peer)

    def y_copy(c):
        return remote(row, c, from_y, c, y_send, y_recv, y_peer)

    def z_copy(c):
        return remote(to_z, c, from_z, c, z_send, z_recv, me + 4)

    def b_copy(c):
        return remote(to_back, c, back, c, b_send, b_recv, x_peer)

    def states(first, j):
        load(0, k_hbm, k, first, j).wait()
        load(1, v_hbm, v, first, j).wait()
        for i in range(PAIR):
            h = first + j * PAIR + i
            at = head_cols(h)
            own[h] = lax.dot_general(
                k[:, at], v[:, at], (((0,), (0,)), ((), ())), preferred_element_type=F32
            )

    @pl.when(zi == 0)
    def _():
        from_z[...] = jnp.zeros_like(from_z)

    squares[...] = jnp.zeros_like(squares)
    below = (zi + planes - 1) // planes
    above = (2 * planes - 2 - zi) // planes
    states(theirs, 0)
    pl.semaphore_wait(barrier, 3 + below + above)
    for i in range(PAIR):
        x_copy(i).start()

    @pl.loop(1, half // PAIR)
    def _(j):
        states(theirs, j)
        for i in range(PAIR):
            x_copy(j * PAIR + i).start()

    @pl.loop(0, half // PAIR)
    def _(j):
        states(mine, j)

    def after_x(c):
        x_copy(c).wait_recv()
        row[c] = own[mine + c] + from_x[c]
        y_copy(c).start()

    def after_y(c):
        y_copy(c).wait_recv()

        @pl.when(zi > 0)
        def _():
            z_copy(c).wait_recv()

        before = from_z[c]

        @pl.when(zi < planes - 1)
        def _():
            to_z[c] = row[c] + from_y[c] + before
            z_copy(c).start()

        zero = jnp.zeros((HD, HD), F32)
        before = before + jnp.where(yi == 1, from_y[c], zero)
        to_back[c] = before + jnp.where(xi == 0, own[mine + c], zero)
        b_copy(c).start()
        cross(mine + c, before + jnp.where(xi == 1, from_x[c], zero))

    def local(h):
        at = head_cols(h)
        for b in range(nb):
            rows = slice(b * BLOCK, (b + 1) * BLOCK)
            qb = q[rows, at]
            total = None
            for u in range(b + 1):
                other = slice(u * BLOCK, (u + 1) * BLOCK)
                scores = lax.dot_general(
                    qb, k[other, at], (((1,), (1,)), ((), ())), preferred_element_type=F32
                )
                if u < b:
                    scores = jnp.where(mask_ref[b, u] == 1, scores, 0.0)
                part = jnp.dot(
                    scores.astype(jnp.bfloat16), v[other, at], preferred_element_type=F32
                )
                total = part if total is None else total + part
            mixed[rows, at] = total

    def cross(h, prefix):
        at = head_cols(h)
        whole = mixed[:, at] + jnp.dot(
            q[:, at], prefix.astype(jnp.bfloat16), preferred_element_type=F32
        )
        mixed[:, at] = whole
        squares[...] += whole * whole

    lag = 1 + zi * 3 // max(planes - 1, 1)

    @pl.loop(0, half + 4 + RETURN_LAG)
    def _(s):
        @pl.when(s < half)
        def _():
            after_x(s)

            @pl.when(lax.rem(s, PAIR) == 0)
            def _():
                load(2, q_hbm, q, mine, s // PAIR).wait()
                load(2, q_hbm, q, theirs, s // PAIR).wait()

            local(mine + s)
            local(theirs + s)

        c = s - lag

        @pl.when(jnp.logical_and(c >= 0, c < half))
        def _():
            after_y(c)

        r = c - RETURN_LAG

        @pl.when(jnp.logical_and(r >= 0, r < half))
        def _():
            b_copy(r).wait_recv()
            cross(theirs + r, back[r])

    tp_copy = pltpu.make_async_remote_copy(
        src_ref=squares, dst_ref=other_squares, send_sem=t_send, recv_sem=t_recv,
        device_id={"tp": 1 - core}, device_id_type=MESH,
    )
    tp_copy.start()

    @pl.loop(0, half)
    def _(c):
        x_copy(c).wait_send()
        y_copy(c).wait_send()
        b_copy(c).wait_send()

        @pl.when(zi < planes - 1)
        def _():
            z_copy(c).wait_send()

    tp_copy.wait()
    rows_out = 64

    @pl.loop(0, tokens // rows_out)
    def _(r):
        at = pl.ds(pl.multiple_of(r * rows_out, rows_out), rows_out)
        total = jnp.sum(squares[at] + other_squares[at], axis=1, keepdims=True)
        scale = lax.rsqrt(total / (width * n_tp) + 1e-6)
        out[at] = (mixed[at] * scale * gain_ref[...]).astype(jnp.bfloat16)


def body(n_seq, n_tp, queries, keys, values, block_mask, gain):
    tokens, width = queries.shape
    heads = width // HD
    half = heads // 2
    sems = pltpu.SemaphoreType.DMA
    vmem = pl.BlockSpec(memory_space=pltpu.VMEM)
    return pl.pallas_call(
        functools.partial(kernel, n_seq, n_tp),
        out_shape=jax.ShapeDtypeStruct((tokens, width), jnp.bfloat16),
        in_specs=[pl.BlockSpec(memory_space=pl.ANY)] * 3
        + [pl.BlockSpec(memory_space=pltpu.SMEM), vmem],
        out_specs=vmem,
        scratch_shapes=[pltpu.VMEM((tokens, width), jnp.bfloat16)] * 3
        + [pltpu.VMEM((tokens, width), F32)]
        + [pltpu.VMEM((heads, HD, HD), F32)]
        + [pltpu.VMEM((half, HD, HD), F32)] * 7
        + [pltpu.VMEM((tokens, HD), F32)] * 2
        + [sems((3, heads // PAIR))]
        + [sems((half,))] * 8
        + [sems, sems],
        compiler_params=pltpu.CompilerParams(
            collective_id=0, has_side_effects=True, vmem_limit_bytes=56 * 1024 * 1024
        ),
    )(queries, keys, values, block_mask, gain.reshape(1, width))


def solution(mesh):
    placed = (P("seq", "tp"), P("seq", "tp"), P("seq", "tp"), P("seq", None), P("tp"))
    return jax.shard_map(
        functools.partial(body, mesh.shape["seq"], mesh.shape["tp"]),
        mesh=mesh, in_specs=placed, out_specs=P("seq", "tp"), check_vma=False,
    )
```

```python
import functools

import jax
import jax.numpy as jnp
from jax import lax
from jax.experimental import pallas as pl
from jax.experimental.pallas import tpu as pltpu
from jax.sharding import PartitionSpec as P

HD = 128
BLOCK = 256
PAIR = 2
ROWS = 128
RETURN_LAG = 3
MESH = pl.DeviceIdType.MESH
F32 = jnp.float32


def kernel(
    n_seq, n_tp,
    q_hbm, k_hbm, v_hbm, mask_ref, mixed, total,
    q, k, v,
    own, from_x, row, from_y, from_z, to_z, to_back, back, squares, other_squares,
    load_sem, x_send, x_recv, y_send, y_recv, z_send, z_recv, b_send, b_recv, t_send, t_recv,
):
    tokens, width = q.shape
    heads = width // HD
    half = heads // 2
    nb = tokens // BLOCK
    planes = n_seq // 4
    me = lax.axis_index("seq")
    core = lax.axis_index("tp")
    xi = lax.rem(me, 2)
    yi = lax.rem(me // 2, 2)
    zi = me // 4
    x_peer = me + 1 - 2 * xi
    y_peer = me + 2 - 4 * yi
    mine = half * xi
    theirs = half - mine

    barrier = pltpu.get_barrier_semaphore()
    pl.semaphore_signal(barrier, inc=1, device_id={"seq": x_peer}, device_id_type=MESH)
    pl.semaphore_signal(barrier, inc=1, device_id={"seq": y_peer}, device_id_type=MESH)
    pl.semaphore_signal(barrier, inc=1, device_id={"tp": 1 - core}, device_id_type=MESH)

    @pl.when(zi > 0)
    def _():
        pl.semaphore_signal(barrier, inc=1, device_id={"seq": me - 4}, device_id_type=MESH)

    @pl.when(zi < planes - 1)
    def _():
        pl.semaphore_signal(barrier, inc=1, device_id={"seq": me + 4}, device_id_type=MESH)

    def head_cols(h, count=1):
        return pl.ds(pl.multiple_of(h * HD, HD), count * HD)

    def load(which, hbm, vmem, first, j):
        at = head_cols(first + j * PAIR, PAIR)
        return pltpu.make_async_copy(
            hbm.at[:, at], vmem.at[:, at], load_sem.at[which, first // PAIR + j]
        )

    for first in (theirs, mine):
        @pl.loop(0, half // PAIR)
        def _(j):
            load(0, k_hbm, k, first, j).start()
            load(1, v_hbm, v, first, j).start()

    def remote(src, at, dst, c, send, recv, peer):
        return pltpu.make_async_remote_copy(
            src_ref=src.at[at], dst_ref=dst.at[c], send_sem=send.at[c], recv_sem=recv.at[c],
            device_id={"seq": peer}, device_id_type=MESH,
        )

    def x_copy(c):
        return remote(own, theirs + c, from_x, c, x_send, x_recv, x_peer)

    def y_copy(c):
        return remote(row, c, from_y, c, y_send, y_recv, y_peer)

    def z_copy(c):
        return remote(to_z, c, from_z, c, z_send, z_recv, me + 4)

    def b_copy(c):
        return remote(to_back, c, back, c, b_send, b_recv, x_peer)

    def states(first, j):
        load(0, k_hbm, k, first, j).wait()
        load(1, v_hbm, v, first, j).wait()
        for i in range(PAIR):
            h = first + j * PAIR + i
            at = head_cols(h)
            own[h] = lax.dot_general(
                k[:, at], v[:, at], (((0,), (0,)), ((), ())), preferred_element_type=F32
            )

    @pl.when(zi == 0)
    def _():
        from_z[...] = jnp.zeros_like(from_z)

    squares[...] = jnp.zeros_like(squares)
    below = (zi + planes - 1) // planes
    above = (2 * planes - 2 - zi) // planes
    states(theirs, 0)
    pl.semaphore_wait(barrier, 3 + below + above)
    for i in range(PAIR):
        x_copy(i).start()

    @pl.loop(1, half // PAIR)
    def _(j):
        states(theirs, j)
        for i in range(PAIR):
            x_copy(j * PAIR + i).start()

    @pl.loop(0, half // PAIR)
    def _(j):
        load(2, q_hbm, q, mine, j).start()
        load(2, q_hbm, q, theirs, j).start()

    @pl.loop(0, half // PAIR)
    def _(j):
        states(mine, j)

    def after_x(c):
        x_copy(c).wait_recv()
        row[c] = own[mine + c] + from_x[c]
        y_copy(c).start()

    def after_y(c):
        y_copy(c).wait_recv()

        @pl.when(zi > 0)
        def _():
            z_copy(c).wait_recv()

        before = from_z[c]

        @pl.when(zi < planes - 1)
        def _():
            to_z[c] = row[c] + from_y[c] + before
            z_copy(c).start()

        zero = jnp.zeros((HD, HD), F32)
        before = before + jnp.where(yi == 1, from_y[c], zero)
        to_back[c] = before + jnp.where(xi == 0, own[mine + c], zero)
        cross(mine + c, before + jnp.where(xi == 1, from_x[c], zero))

    def local(h):
        at = head_cols(h)
        for b in range(nb):
            rows = slice(b * BLOCK, (b + 1) * BLOCK)
            qb = q[rows, at]
            part_sum = None
            for u in range(b + 1):
                other = slice(u * BLOCK, (u + 1) * BLOCK)
                scores = lax.dot_general(
                    qb, k[other, at], (((1,), (1,)), ((), ())), preferred_element_type=F32
                )
                if u < b:
                    scores = jnp.where(mask_ref[b, u] == 1, scores, 0.0)
                part = jnp.dot(
                    scores.astype(jnp.bfloat16), v[other, at], preferred_element_type=F32
                )
                part_sum = part if part_sum is None else part_sum + part
            mixed[rows, at] = part_sum

    def cross(h, prefix):
        at = head_cols(h)
        whole = mixed[:, at] + jnp.dot(
            q[:, at], prefix.astype(jnp.bfloat16), preferred_element_type=F32
        )
        mixed[:, at] = whole
        squares[...] += whole * whole

    lag = 1 + zi * 3 // max(planes - 1, 1)
    hold = (planes - 1 - zi) * 5 // max(planes - 1, 1)

    @pl.loop(0, half + 6 + RETURN_LAG)
    def _(s):
        @pl.when(s < half)
        def _():
            after_x(s)

            @pl.when(lax.rem(s, PAIR) == 0)
            def _():
                load(2, q_hbm, q, mine, s // PAIR).wait()
                load(2, q_hbm, q, theirs, s // PAIR).wait()

            local(mine + s)
            local(theirs + s)

        c = s - lag

        @pl.when(jnp.logical_and(c >= 0, c < half))
        def _():
            after_y(c)

        g = c - hold

        @pl.when(jnp.logical_and(g >= 0, g < half))
        def _():
            b_copy(g).start()

        r = g - RETURN_LAG

        @pl.when(jnp.logical_and(r >= 0, r < half))
        def _():
            b_copy(r).wait_recv()
            cross(theirs + r, back[r])

    tp_copy = pltpu.make_async_remote_copy(
        src_ref=squares, dst_ref=other_squares, send_sem=t_send, recv_sem=t_recv,
        device_id={"tp": 1 - core}, device_id_type=MESH,
    )
    tp_copy.start()

    @pl.loop(0, half)
    def _(c):
        x_copy(c).wait_send()
        y_copy(c).wait_send()
        b_copy(c).wait_send()

        @pl.when(zi < planes - 1)
        def _():
            z_copy(c).wait_send()

    tp_copy.wait()
    total[...] = squares[...] + other_squares[...]


def norm_kernel(n_tp, mixed, total, gain_ref, out_hbm, staged, sem):
    tokens, width = mixed.shape
    steps = tokens // ROWS

    def rows(r):
        return pl.ds(pl.multiple_of(r * ROWS, ROWS), ROWS)

    def out_copy(r):
        return pltpu.make_async_copy(staged.at[rows(r)], out_hbm.at[rows(r)], sem.at[r])

    @pl.loop(0, steps)
    def _(r):
        at = rows(r)
        mean = jnp.sum(total[at], axis=1, keepdims=True) / (width * n_tp)
        scale = lax.rsqrt(mean + 1e-6)
        staged[at] = (mixed[at] * scale * gain_ref[...]).astype(jnp.bfloat16)
        out_copy(r).start()

    @pl.loop(0, steps)
    def _(r):
        out_copy(r).wait()


def body(n_seq, n_tp, queries, keys, values, block_mask, gain):
    tokens, width = queries.shape
    heads = width // HD
    half = heads // 2
    sems = pltpu.SemaphoreType.DMA
    vmem = pl.BlockSpec(memory_space=pltpu.VMEM)
    mixed, total = pl.pallas_call(
        functools.partial(kernel, n_seq, n_tp),
        out_shape=(
            jax.ShapeDtypeStruct((tokens, width), F32),
            jax.ShapeDtypeStruct((tokens, HD), F32),
        ),
        in_specs=[pl.BlockSpec(memory_space=pl.ANY)] * 3
        + [pl.BlockSpec(memory_space=pltpu.SMEM)],
        out_specs=(vmem, vmem),
        scratch_shapes=[pltpu.VMEM((tokens, width), jnp.bfloat16)] * 3
        + [pltpu.VMEM((heads, HD, HD), F32)]
        + [pltpu.VMEM((half, HD, HD), F32)] * 7
        + [pltpu.VMEM((tokens, HD), F32)] * 2
        + [sems((3, heads // PAIR))]
        + [sems((half,))] * 8
        + [sems, sems],
        compiler_params=pltpu.CompilerParams(
            collective_id=0, has_side_effects=True, vmem_limit_bytes=56 * 1024 * 1024
        ),
    )(queries, keys, values, block_mask)
    return pl.pallas_call(
        functools.partial(norm_kernel, n_tp),
        out_shape=jax.ShapeDtypeStruct((tokens, width), jnp.bfloat16),
        in_specs=[vmem] * 3,
        out_specs=pl.BlockSpec(memory_space=pl.ANY),
        scratch_shapes=[pltpu.VMEM((tokens, width), jnp.bfloat16), sems((tokens // ROWS,))],
    )(mixed, total, gain.reshape(1, width))


def solution(mesh):
    placed = (P("seq", "tp"), P("seq", "tp"), P("seq", "tp"), P("seq", None), P("tp"))
    return jax.shard_map(
        functools.partial(body, mesh.shape["seq"], mesh.shape["tp"]),
        mesh=mesh, in_specs=placed, out_specs=P("seq", "tp"), check_vma=False,
    )
```

```python
import functools

import jax
import jax.numpy as jnp
from jax import lax
from jax.experimental import pallas as pl
from jax.experimental.pallas import tpu as pltpu
from jax.sharding import PartitionSpec as P

HD = 128
BLOCK = 256
PAIR = 2
SPLIT = 2
CUT = HD // SPLIT
ROWS = 128
RETURN_LAG = 4
LAG = 3
HOP = 3
HOLD = 10
MESH = pl.DeviceIdType.MESH
F32 = jnp.float32


def kernel(
    n_seq, n_tp,
    q_hbm, k_hbm, v_hbm, mask_ref, mixed, total,
    q, k, v,
    own, from_x, row, from_y, from_z, to_z, to_back, back, prefix, squares, other_squares,
    load_sem, x_send, x_recv, y_send, y_recv, z_send, z_recv, b_send, b_recv, t_send, t_recv,
):
    tokens, width = q.shape
    heads = width // HD
    half = heads // 2
    pieces = half * SPLIT
    nb = tokens // BLOCK
    planes = n_seq // 4
    me = lax.axis_index("seq")
    core = lax.axis_index("tp")
    xi = lax.rem(me, 2)
    yi = lax.rem(me // 2, 2)
    zi = me // 4
    x_peer = me + 1 - 2 * xi
    y_peer = me + 2 - 4 * yi
    mine = half * xi
    theirs = half - mine

    barrier = pltpu.get_barrier_semaphore()
    pl.semaphore_signal(barrier, inc=1, device_id={"seq": x_peer}, device_id_type=MESH)
    pl.semaphore_signal(barrier, inc=1, device_id={"seq": y_peer}, device_id_type=MESH)
    pl.semaphore_signal(barrier, inc=1, device_id={"tp": 1 - core}, device_id_type=MESH)

    @pl.when(zi > 0)
    def _():
        pl.semaphore_signal(barrier, inc=1, device_id={"seq": me - 4}, device_id_type=MESH)

    @pl.when(zi < planes - 1)
    def _():
        pl.semaphore_signal(barrier, inc=1, device_id={"seq": me + 4}, device_id_type=MESH)

    def head_cols(h, count=1):
        return pl.ds(pl.multiple_of(h * HD, HD), count * HD)

    def load(which, hbm, vmem, first, j):
        at = head_cols(first + j * PAIR, PAIR)
        return pltpu.make_async_copy(
            hbm.at[:, at], vmem.at[:, at], load_sem.at[which, first // PAIR + j]
        )

    for first in (theirs, mine):
        @pl.loop(0, half // PAIR)
        def _(j):
            load(0, k_hbm, k, first, j).start()
            load(1, v_hbm, v, first, j).start()

    def remote(src, at, dst, c, send, recv, peer):
        return pltpu.make_async_remote_copy(
            src_ref=src.at[at], dst_ref=dst.at[c], send_sem=send.at[c], recv_sem=recv.at[c],
            device_id={"seq": peer}, device_id_type=MESH,
        )

    def x_copy(c):
        return remote(own, theirs * SPLIT + c, from_x, c, x_send, x_recv, x_peer)

    def y_copy(c):
        return remote(row, c, from_y, c, y_send, y_recv, y_peer)

    def z_copy(c):
        return remote(to_z, c, from_z, c, z_send, z_recv, me + 4)

    def b_copy(c):
        return remote(to_back, c, back, c, b_send, b_recv, x_peer)

    def states(first, j):
        load(0, k_hbm, k, first, j).wait()
        load(1, v_hbm, v, first, j).wait()
        for i in range(PAIR):
            h = first + j * PAIR + i
            at = head_cols(h)
            state = lax.dot_general(
                k[:, at], v[:, at], (((0,), (0,)), ((), ())), preferred_element_type=F32
            )
            own[pl.ds(h * SPLIT, SPLIT)] = state.reshape(SPLIT, CUT, HD)

    @pl.when(zi == 0)
    def _():
        from_z[...] = jnp.zeros_like(from_z)

    squares[...] = jnp.zeros_like(squares)
    below = (zi + planes - 1) // planes
    above = (2 * planes - 2 - zi) // planes
    states(theirs, 0)
    pl.semaphore_wait(barrier, 3 + below + above)
    for i in range(PAIR * SPLIT):
        x_copy(i).start()

    @pl.loop(1, half // PAIR)
    def _(j):
        states(theirs, j)
        for i in range(PAIR * SPLIT):
            x_copy(j * PAIR * SPLIT + i).start()

    @pl.loop(0, half // PAIR)
    def _(j):
        load(2, q_hbm, q, mine, j).start()
        load(2, q_hbm, q, theirs, j).start()

    @pl.loop(0, half // PAIR)
    def _(j):
        states(mine, j)

    def after_x(c):
        x_copy(c).wait_recv()
        row[c] = own[mine * SPLIT + c] + from_x[c]
        y_copy(c).start()

    def after_y(c):
        y_copy(c).wait_recv()

        @pl.when(zi > 0)
        def _():
            z_copy(c).wait_recv()

        before = from_z[c]

        @pl.when(zi < planes - 1)
        def _():
            to_z[c] = row[c] + from_y[c] + before
            z_copy(c).start()

        zero = jnp.zeros((CUT, HD), F32)
        before = before + jnp.where(yi == 1, from_y[c], zero)
        to_back[c] = before + jnp.where(xi == 0, own[mine * SPLIT + c], zero)
        prefix[c] = before + jnp.where(xi == 1, from_x[c], zero)

        @pl.when(lax.rem(c, SPLIT) == SPLIT - 1)
        def _():
            cross(mine, c // SPLIT, prefix)

    def local(h):
        at = head_cols(h)
        for b in range(nb):
            rows = slice(b * BLOCK, (b + 1) * BLOCK)
            qb = q[rows, at]
            part_sum = None
            for u in range(b + 1):
                other = slice(u * BLOCK, (u + 1) * BLOCK)
                scores = lax.dot_general(
                    qb, k[other, at], (((1,), (1,)), ((), ())), preferred_element_type=F32
                )
                if u < b:
                    scores = jnp.where(mask_ref[b, u] == 1, scores, 0.0)
                part = jnp.dot(
                    scores.astype(jnp.bfloat16), v[other, at], preferred_element_type=F32
                )
                part_sum = part if part_sum is None else part_sum + part
            mixed[rows, at] = part_sum

    def cross(first, j, held):
        at = head_cols(first + j)
        whole_state = held[pl.ds(j * SPLIT, SPLIT)].reshape(HD, HD)
        whole = mixed[:, at] + jnp.dot(
            q[:, at], whole_state.astype(jnp.bfloat16), preferred_element_type=F32
        )
        mixed[:, at] = whole
        squares[...] += whole * whole

    lag = LAG + zi * 3 * HOP // max(planes - 1, 1)
    hold = (planes - 1 - zi) * HOLD // max(planes - 1, 1)

    @pl.loop(0, pieces + LAG + 3 * HOP + HOLD + RETURN_LAG)
    def _(s):
        @pl.when(s < pieces)
        def _():
            after_x(s)

            @pl.when(lax.rem(s, SPLIT * PAIR) == 0)
            def _():
                load(2, q_hbm, q, mine, s // (SPLIT * PAIR)).wait()
                load(2, q_hbm, q, theirs, s // (SPLIT * PAIR)).wait()

            local(lax.rem(s, SPLIT) * theirs + (1 - lax.rem(s, SPLIT)) * mine + s // SPLIT)

        c = s - lag

        @pl.when(jnp.logical_and(c >= 0, c < pieces))
        def _():
            after_y(c)

        g = c - hold

        @pl.when(jnp.logical_and(g >= 0, g < pieces))
        def _():
            b_copy(g).start()

        r = g - RETURN_LAG

        @pl.when(jnp.logical_and(r >= 0, r < pieces))
        def _():
            b_copy(r).wait_recv()

            @pl.when(lax.rem(r, SPLIT) == SPLIT - 1)
            def _():
                cross(theirs, r // SPLIT, back)

    tp_copy = pltpu.make_async_remote_copy(
        src_ref=squares, dst_ref=other_squares, send_sem=t_send, recv_sem=t_recv,
        device_id={"tp": 1 - core}, device_id_type=MESH,
    )
    tp_copy.start()

    @pl.loop(0, pieces)
    def _(c):
        x_copy(c).wait_send()
        y_copy(c).wait_send()
        b_copy(c).wait_send()

        @pl.when(zi < planes - 1)
        def _():
            z_copy(c).wait_send()

    tp_copy.wait()
    total[...] = squares[...] + other_squares[...]


def norm_kernel(n_tp, mixed, total, gain_ref, out_hbm, staged, sem):
    tokens, width = mixed.shape
    steps = tokens // ROWS

    def rows(r):
        return pl.ds(pl.multiple_of(r * ROWS, ROWS), ROWS)

    def out_copy(r):
        return pltpu.make_async_copy(staged.at[rows(r)], out_hbm.at[rows(r)], sem.at[r])

    @pl.loop(0, steps)
    def _(r):
        at = rows(r)
        mean = jnp.sum(total[at], axis=1, keepdims=True) / (width * n_tp)
        scale = lax.rsqrt(mean + 1e-6)
        staged[at] = (mixed[at] * scale * gain_ref[...]).astype(jnp.bfloat16)
        out_copy(r).start()

    @pl.loop(0, steps)
    def _(r):
        out_copy(r).wait()


def body(n_seq, n_tp, queries, keys, values, block_mask, gain):
    tokens, width = queries.shape
    heads = width // HD
    half = heads // 2
    sems = pltpu.SemaphoreType.DMA
    vmem = pl.BlockSpec(memory_space=pltpu.VMEM)
    mixed, total = pl.pallas_call(
        functools.partial(kernel, n_seq, n_tp),
        out_shape=(
            jax.ShapeDtypeStruct((tokens, width), F32),
            jax.ShapeDtypeStruct((tokens, HD), F32),
        ),
        in_specs=[pl.BlockSpec(memory_space=pl.ANY)] * 3
        + [pl.BlockSpec(memory_space=pltpu.SMEM)],
        out_specs=(vmem, vmem),
        scratch_shapes=[pltpu.VMEM((tokens, width), jnp.bfloat16)] * 3
        + [pltpu.VMEM((heads * SPLIT, CUT, HD), F32)]
        + [pltpu.VMEM((half * SPLIT, CUT, HD), F32)] * 8
        + [pltpu.VMEM((tokens, HD), F32)] * 2
        + [sems((3, heads // PAIR))]
        + [sems((half * SPLIT,))] * 8
        + [sems, sems],
        compiler_params=pltpu.CompilerParams(
            collective_id=0, has_side_effects=True, vmem_limit_bytes=56 * 1024 * 1024
        ),
    )(queries, keys, values, block_mask)
    return pl.pallas_call(
        functools.partial(norm_kernel, n_tp),
        out_shape=jax.ShapeDtypeStruct((tokens, width), jnp.bfloat16),
        in_specs=[vmem] * 3,
        out_specs=pl.BlockSpec(memory_space=pl.ANY),
        scratch_shapes=[pltpu.VMEM((tokens, width), jnp.bfloat16), sems((tokens // ROWS,))],
    )(mixed, total, gain.reshape(1, width))


def solution(mesh):
    placed = (P("seq", "tp"), P("seq", "tp"), P("seq", "tp"), P("seq", None), P("tp"))
    return jax.shard_map(
        functools.partial(body, mesh.shape["seq"], mesh.shape["tp"]),
        mesh=mesh, in_specs=placed, out_specs=P("seq", "tp"), check_vma=False,
    )
```

```python
import functools

import jax
import jax.numpy as jnp
from jax import lax
from jax.experimental import pallas as pl
from jax.experimental.pallas import tpu as pltpu
from jax.sharding import PartitionSpec as P

HD = 128
BLOCK = 256
PAIR = 2
SPLIT = 2
CUT = HD // SPLIT
ROWS = 128
RETURN_LAG = 4
LAG = 4
HOP = 3
HOLD = 10
MESH = pl.DeviceIdType.MESH
F32 = jnp.float32


def kernel(
    n_seq, n_tp,
    q_hbm, k_hbm, v_hbm, mask_ref, mixed, total,
    q, k, v,
    own, from_x, row, from_y, from_z, to_z, to_back, back, prefix, squares, other_squares,
    load_sem, x_send, x_recv, y_send, y_recv, z_send, z_recv, b_send, b_recv, t_send, t_recv,
):
    tokens, width = q.shape
    heads = width // HD
    half = heads // 2
    pieces = half * SPLIT
    nb = tokens // BLOCK
    planes = n_seq // 4
    me = lax.axis_index("seq")
    core = lax.axis_index("tp")
    xi = lax.rem(me, 2)
    yi = lax.rem(me // 2, 2)
    zi = me // 4
    x_peer = me + 1 - 2 * xi
    y_peer = me + 2 - 4 * yi
    mine = half * xi
    theirs = half - mine

    barrier = pltpu.get_barrier_semaphore()
    pl.semaphore_signal(barrier, inc=1, device_id={"seq": x_peer}, device_id_type=MESH)
    pl.semaphore_signal(barrier, inc=1, device_id={"seq": y_peer}, device_id_type=MESH)
    pl.semaphore_signal(barrier, inc=1, device_id={"tp": 1 - core}, device_id_type=MESH)

    @pl.when(zi > 0)
    def _():
        pl.semaphore_signal(barrier, inc=1, device_id={"seq": me - 4}, device_id_type=MESH)

    @pl.when(zi < planes - 1)
    def _():
        pl.semaphore_signal(barrier, inc=1, device_id={"seq": me + 4}, device_id_type=MESH)

    def head_cols(h, count=1):
        return pl.ds(pl.multiple_of(h * HD, HD), count * HD)

    def load(which, hbm, vmem, first, j):
        at = head_cols(first + j * PAIR, PAIR)
        return pltpu.make_async_copy(
            hbm.at[:, at], vmem.at[:, at], load_sem.at[which, first // PAIR + j]
        )

    for first in (theirs, mine):
        @pl.loop(0, half // PAIR)
        def _(j):
            load(0, k_hbm, k, first, j).start()
            load(1, v_hbm, v, first, j).start()

    def remote(src, at, dst, c, send, recv, peer):
        return pltpu.make_async_remote_copy(
            src_ref=src.at[at], dst_ref=dst.at[c], send_sem=send.at[c], recv_sem=recv.at[c],
            device_id={"seq": peer}, device_id_type=MESH,
        )

    def x_copy(c):
        return remote(own, theirs * SPLIT + c, from_x, c, x_send, x_recv, x_peer)

    def y_copy(c):
        return remote(row, c, from_y, c, y_send, y_recv, y_peer)

    def z_copy(c):
        return remote(to_z, c, from_z, c, z_send, z_recv, me + 4)

    def b_copy(c):
        return remote(to_back, c, back, c, b_send, b_recv, x_peer)

    def states(first, j):
        load(0, k_hbm, k, first, j).wait()
        load(1, v_hbm, v, first, j).wait()
        for i in range(PAIR):
            h = first + j * PAIR + i
            at = head_cols(h)
            state = lax.dot_general(
                k[:, at], v[:, at], (((0,), (0,)), ((), ())), preferred_element_type=F32
            )
            own[pl.ds(h * SPLIT, SPLIT)] = state.reshape(SPLIT, CUT, HD)

    @pl.when(zi == 0)
    def _():
        from_z[...] = jnp.zeros_like(from_z)

    squares[...] = jnp.zeros_like(squares)
    below = (zi + planes - 1) // planes
    above = (2 * planes - 2 - zi) // planes
    states(theirs, 0)
    pl.semaphore_wait(barrier, 3 + below + above)
    for i in range(PAIR * SPLIT):
        x_copy(i).start()

    @pl.loop(1, half // PAIR)
    def _(j):
        states(theirs, j)
        for i in range(PAIR * SPLIT):
            x_copy(j * PAIR * SPLIT + i).start()

    @pl.loop(0, half // PAIR)
    def _(j):
        load(2, q_hbm, q, mine, j).start()
        load(2, q_hbm, q, theirs, j).start()

    @pl.loop(0, half // PAIR)
    def _(j):
        states(mine, j)

    def after_x(c):
        x_copy(c).wait_recv()
        row[c] = own[mine * SPLIT + c] + from_x[c]
        y_copy(c).start()

    def after_y(c):
        y_copy(c).wait_recv()

        @pl.when(zi > 0)
        def _():
            z_copy(c).wait_recv()

        before = from_z[c]

        @pl.when(zi < planes - 1)
        def _():
            to_z[c] = row[c] + from_y[c] + before
            z_copy(c).start()

        zero = jnp.zeros((CUT, HD), F32)
        before = before + jnp.where(yi == 1, from_y[c], zero)
        to_back[c] = before + jnp.where(xi == 0, own[mine * SPLIT + c], zero)
        prefix[c] = before + jnp.where(xi == 1, from_x[c], zero)

        @pl.when(lax.rem(c, SPLIT) == SPLIT - 1)
        def _():
            cross(mine, c // SPLIT, prefix)

    def local(h):
        at = head_cols(h)
        for b in range(nb):
            rows = slice(b * BLOCK, (b + 1) * BLOCK)
            qb = q[rows, at]
            part_sum = None
            for u in range(b + 1):
                other = slice(u * BLOCK, (u + 1) * BLOCK)
                scores = lax.dot_general(
                    qb, k[other, at], (((1,), (1,)), ((), ())), preferred_element_type=F32
                )
                if u < b:
                    scores = jnp.where(mask_ref[b, u] == 1, scores, 0.0)
                part = jnp.dot(
                    scores.astype(jnp.bfloat16), v[other, at], preferred_element_type=F32
                )
                part_sum = part if part_sum is None else part_sum + part
            mixed[rows, at] = part_sum

    def cross(first, j, held):
        at = head_cols(first + j)
        whole_state = held[pl.ds(j * SPLIT, SPLIT)].reshape(HD, HD)
        whole = mixed[:, at] + jnp.dot(
            q[:, at], whole_state.astype(jnp.bfloat16), preferred_element_type=F32
        )
        mixed[:, at] = whole
        squares[...] += whole * whole

    lag = LAG + zi * 3 * HOP // max(planes - 1, 1)
    hold = (planes - 1 - zi) * HOLD // max(planes - 1, 1)

    @pl.loop(0, pieces + LAG + 3 * HOP + HOLD + RETURN_LAG)
    def _(s):
        @pl.when(s < pieces)
        def _():
            after_x(s)

            @pl.when(lax.rem(s, SPLIT * PAIR) == 0)
            def _():
                load(2, q_hbm, q, mine, s // (SPLIT * PAIR)).wait()
                load(2, q_hbm, q, theirs, s // (SPLIT * PAIR)).wait()

            local(lax.rem(s, SPLIT) * theirs + (1 - lax.rem(s, SPLIT)) * mine + s // SPLIT)

        c = s - lag

        @pl.when(jnp.logical_and(c >= 0, c < pieces))
        def _():
            after_y(c)

        g = c - hold

        @pl.when(jnp.logical_and(g >= 0, g < pieces))
        def _():
            b_copy(g).start()

        r = g - RETURN_LAG

        @pl.when(jnp.logical_and(r >= 0, r < pieces))
        def _():
            b_copy(r).wait_recv()

            @pl.when(lax.rem(r, SPLIT) == SPLIT - 1)
            def _():
                cross(theirs, r // SPLIT, back)

    tp_copy = pltpu.make_async_remote_copy(
        src_ref=squares, dst_ref=other_squares, send_sem=t_send, recv_sem=t_recv,
        device_id={"tp": 1 - core}, device_id_type=MESH,
    )
    tp_copy.start()

    @pl.loop(0, pieces)
    def _(c):
        x_copy(c).wait_send()
        y_copy(c).wait_send()
        b_copy(c).wait_send()

        @pl.when(zi < planes - 1)
        def _():
            z_copy(c).wait_send()

    tp_copy.wait()
    total[...] = squares[...] + other_squares[...]


def norm_kernel(n_tp, mixed, total, gain_ref, out_hbm, staged, sem):
    tokens, width = mixed.shape
    steps = tokens // ROWS

    def rows(r):
        return pl.ds(pl.multiple_of(r * ROWS, ROWS), ROWS)

    def out_copy(r):
        return pltpu.make_async_copy(staged.at[rows(r)], out_hbm.at[rows(r)], sem.at[r])

    @pl.loop(0, steps)
    def _(r):
        at = rows(r)
        mean = jnp.sum(total[at], axis=1, keepdims=True) / (width * n_tp)
        scale = lax.rsqrt(mean + 1e-6)
        staged[at] = (mixed[at] * scale * gain_ref[...]).astype(jnp.bfloat16)
        out_copy(r).start()

    @pl.loop(0, steps)
    def _(r):
        out_copy(r).wait()


def body(n_seq, n_tp, queries, keys, values, block_mask, gain):
    tokens, width = queries.shape
    heads = width // HD
    half = heads // 2
    sems = pltpu.SemaphoreType.DMA
    vmem = pl.BlockSpec(memory_space=pltpu.VMEM)
    mixed, total = pl.pallas_call(
        functools.partial(kernel, n_seq, n_tp),
        out_shape=(
            jax.ShapeDtypeStruct((tokens, width), F32),
            jax.ShapeDtypeStruct((tokens, HD), F32),
        ),
        in_specs=[pl.BlockSpec(memory_space=pl.ANY)] * 3
        + [pl.BlockSpec(memory_space=pltpu.SMEM)],
        out_specs=(vmem, vmem),
        scratch_shapes=[pltpu.VMEM((tokens, width), jnp.bfloat16)] * 3
        + [pltpu.VMEM((heads * SPLIT, CUT, HD), F32)]
        + [pltpu.VMEM((half * SPLIT, CUT, HD), F32)] * 8
        + [pltpu.VMEM((tokens, HD), F32)] * 2
        + [sems((3, heads // PAIR))]
        + [sems((half * SPLIT,))] * 8
        + [sems, sems],
        compiler_params=pltpu.CompilerParams(
            collective_id=0, has_side_effects=True, vmem_limit_bytes=56 * 1024 * 1024
        ),
    )(queries, keys, values, block_mask)
    return pl.pallas_call(
        functools.partial(norm_kernel, n_tp),
        out_shape=jax.ShapeDtypeStruct((tokens, width), jnp.bfloat16),
        in_specs=[vmem] * 3,
        out_specs=pl.BlockSpec(memory_space=pl.ANY),
        scratch_shapes=[pltpu.VMEM((tokens, width), jnp.bfloat16), sems((tokens // ROWS,))],
    )(mixed, total, gain.reshape(1, width))


def solution(mesh):
    placed = (P("seq", "tp"), P("seq", "tp"), P("seq", "tp"), P("seq", None), P("tp"))
    return jax.shard_map(
        functools.partial(body, mesh.shape["seq"], mesh.shape["tp"]),
        mesh=mesh, in_specs=placed, out_specs=P("seq", "tp"), check_vma=False,
    )
```
